32 devices in a mesh: group: 2 (over x), ctx: 8 (over z, y), tp: 2 (over core).
Axes of the slice: x: 2, y: 2, z: 4, core: 2. Of those that a mesh axis runs over, the one named last changes fastest.
Arguments:
- query_proj: bfloat16 [2048, 8192], P(('group', 'ctx'), 'tp'), parts along dimension 0, may hold values from -6 to 6
- key_proj: bfloat16 [2048, 8192], P(('group', 'ctx'), 'tp'), parts along dimension 0, may hold values from -6 to 6
- value_proj: bfloat16 [2048, 8192], P(('group', 'ctx'), 'tp'), parts along dimension 0, may hold values from -6 to 6
- genome_ids: int32 [2048], P('group'), parts along dimension 0, may hold values from 0 to 3, never falling along the last dimension, each value on 1 to 512 neighbouring positions
- filters: float32 [512, 128], P('tp'), may hold values from -0.5 to 0.5
- out_weight: bfloat16 [8192, 8192], P('tp', 'ctx'), may hold values from -0.0625 to 0.0625
- out_grad: bfloat16 [2048, 8192], P(('group', 'ctx'), 'tp'), parts along dimension 0, may hold values from -6 to 6
Outputs:
- query_grad: bfloat16 [2048, 8192], P(('group', 'ctx'), 'tp'), parts along dimension 0
- key_grad: bfloat16 [2048, 8192], P(('group', 'ctx'), 'tp'), parts along dimension 0
- value_grad: bfloat16 [2048, 8192], P(('group', 'ctx'), 'tp'), parts along dimension 0
- filter_grad: float32 [1024, 128], P(('group', 'tp')), parts along dimension 0
The draws below stay inside these ranges and needn't reach their ends.
There are 2 independent parts, one for each index of `group`. The reference program is written for one: setup_inputs(seed, part) draws one part's arguments, and reference() takes and returns one part's arrays. A program takes and returns all parts, laid end to end along the dimension named above; an argument that names none is the same for every part. Nothing has to cross between parts.
Inputs may be any that keep to these rules, and one draw needn't show every extreme that they name: `genome_ids`: genome ids never fall along the rows; every genome covers 1 to 512 consecutive rows, and one covers exactly 512.
All inputs are finite; a program needn't handle non-finite values.
Results may differ from the reference program's by a relative error of at most 0.017.
Values may be sent and summed in bfloat16 or wider, within the bound.
A program may use at most 192 MiB of HBM per device.

```python
import math
import jax
import jax.numpy as jnp
import numpy as np
from jax import lax

D = 8192
TAPS = 128
GROUP_CH = 16
GROUPS = 512
TOKENS = 1024
N_CTX = 8


def block_scale(stream_key, extent, cuts, smallest, top_value):
    level = 1.0
    for position, shards_of in cuts:
        heights = jax.random.uniform(jax.random.fold_in(jax.random.fold_in(stream_key, 6), position), (shards_of,), jnp.float32, smallest / len(cuts), top_value / len(cuts))
        level = level * jnp.repeat(jnp.exp(heights), extent[position] // shards_of).reshape((-1,) + (1,) * (len(extent) - 1 - position))
    return level


def profile(number_of, total, limit, lean):
    weights = [(1 << 20) // math.isqrt(rank ** lean) + 1 for rank in range(2, number_of + 1)]
    spare, counts = total - limit - (number_of - 1), [1] * (number_of - 1)
    while spare > 0:
        free = [i for i in range(number_of - 1) if counts[i] < limit]
        whole, remaining = sum([weights[i] for i in free]), spare
        for i in free:
            extra = min(limit - counts[i], max(1, remaining * weights[i] // whole), spare)
            counts[i] = counts[i] + extra
            spare = spare - extra
    return np.array([limit] + counts)


def uneven(own_key, amount, total, most, lean):
    if amount == 2:
        one = jax.random.randint(own_key, (), max(1, total - most), min(most, total - 1) + 1)
        return jnp.stack([one, total - one])
    tallies = jnp.asarray(profile(amount, total, most, lean), jnp.int32)
    twos = (amount - 1) // 2
    source_of, sink = tallies[1:1 + 2 * twos:2], tallies[2:2 + 2 * twos:2]
    slack = jnp.minimum(source_of - 1, most - sink)
    moved = jax.random.randint(jax.random.fold_in(own_key, 1), (twos,), 0, 1 << 20) % (slack + 1)
    tallies = tallies.at[1:1 + 2 * twos:2].set(source_of - moved).at[2:2 + 2 * twos:2].set(sink + moved)
    return tallies[jax.random.permutation(jax.random.fold_in(own_key, 2), amount)]


def normal_values(rng, extent, scale, most, cuts=(), kind=jnp.bfloat16):
    level = block_scale(rng, extent, cuts, -0.22, 0.18) if cuts else 1.0
    result = jax.random.normal(rng, extent, jnp.float32) * scale * level
    return jnp.minimum(jnp.maximum(result, -most), most).astype(kind)


def setup_inputs(seed: int = 0, part: int = 0) -> dict:
    keys = jax.random.split(jax.random.key(seed), 8)
    part_splits = jax.random.split(jax.random.fold_in(keys[7], part), 8)
    return {
        "query_proj": normal_values(part_splits[0], (TOKENS, D), 1.0, 6.0, ((0, 8), (1, 2))),
        "key_proj": normal_values(part_splits[1], (TOKENS, D), 1.0, 6.0, ((0, 8), (1, 2))),
        "value_proj": normal_values(part_splits[2], (TOKENS, D), 1.0, 6.0, ((0, 8), (1, 2))),
        "genome_ids": jnp.searchsorted(jnp.cumsum(uneven(part_splits[3], 4, TOKENS, TOKENS // 2, 2)), jnp.arange(TOKENS), side="right").astype(jnp.int32),
        "filters": normal_values(keys[4], (GROUPS, TAPS), TAPS ** -0.5, 0.5, ((0, 2),), jnp.float32),
        "out_weight": normal_values(keys[5], (D, D), D ** -0.5, 0.0625, ((0, 2), (1, 8))),
        "out_grad": normal_values(part_splits[6], (TOKENS, D), 1.0, 6.0, ((0, 8), (1, 2))),
    }


def rounded(source):
    return lax.optimization_barrier(source.astype(jnp.bfloat16)).astype(jnp.float32)


def lag_tables(filt_vals, tap_count):
    row_pos = np.arange(tap_count)[:, None]
    col_pos = np.arange(2 * tap_count)[None, :]
    tables = []
    for offsets in (row_pos + tap_count - col_pos, col_pos - row_pos):
        inside = (offsets >= 0) & (offsets < tap_count)
        picked = jnp.take(filt_vals, np.clip(offsets, 0, tap_count - 1).reshape(-1), axis=1)
        picked = picked.reshape(filt_vals.shape[0], tap_count, 2 * tap_count)
        tables.append(jnp.where(inside[None], picked, jnp.zeros_like(picked)))
    return tables[0], tables[1]


def fold_lags(product, tap_count):
    group_count = product.shape[0]
    flat = product.reshape(group_count, 2 * tap_count * tap_count)
    flat = jnp.concatenate([flat, jnp.zeros((group_count, tap_count), flat.dtype)], 1)
    skewed = flat.reshape(group_count, tap_count, 2 * tap_count + 1)
    return jnp.flip(jnp.sum(skewed[:, :, 1:tap_count + 1], axis=1), axis=1)


def reference(query_proj, key_proj, value_proj, genome_ids, filters, out_weight, out_grad):
    highest = lax.Precision.HIGHEST
    key_f32 = key_proj.astype(jnp.float32)
    value_f32 = value_proj.astype(jnp.float32)
    mixed = rounded(key_f32 * value_f32)
    fwd_table, back_table = lag_tables(rounded(filters), TAPS)
    pad_ids = jnp.full((TAPS,), -1, jnp.int32)
    ids_pad = jnp.concatenate([pad_ids, genome_ids.astype(jnp.int32), pad_ids])
    zero_rows = jnp.zeros((TAPS, D), jnp.float32)
    mixed_ext = jnp.concatenate([zero_rows, mixed], 0)
    width_ctx = D // N_CTX

    def dz_step(block_index, running):
        first_col = (block_index * width_ctx).astype(jnp.int32)
        grad_cols = lax.dynamic_slice_in_dim(out_grad, first_col, width_ctx, 1)
        weight_cols = lax.dynamic_slice_in_dim(out_weight, first_col, width_ctx, 1)
        return running + rounded(jnp.dot(grad_cols, weight_cols.T, preferred_element_type=jnp.float32))

    summed = lax.fori_loop(0, N_CTX, dz_step, jnp.zeros((TOKENS, D), jnp.float32))
    dz_vals = rounded(summed)

    def conv_step(block_index, conv_all):
        first_row = (block_index * TAPS).astype(jnp.int32)
        window = lax.dynamic_slice_in_dim(mixed_ext, first_row, 2 * TAPS, 0)
        ids_rows = lax.dynamic_slice_in_dim(ids_pad, first_row + TAPS, TAPS, 0)
        ids_prev = lax.dynamic_slice_in_dim(ids_pad, first_row, 2 * TAPS, 0)
        same_prev = (ids_rows[:, None] == ids_prev[None, :]).astype(jnp.float32)
        block_out = jnp.einsum("gtw,wgc->tgc", fwd_table * same_prev[None],
                               window.reshape(2 * TAPS, GROUPS, GROUP_CH), precision=highest)
        return lax.dynamic_update_slice_in_dim(conv_all, block_out.reshape(TAPS, D), first_row, 0)

    conv = lax.fori_loop(0, TOKENS // TAPS, conv_step, jnp.zeros((TOKENS, D), jnp.float32))
    query_grad = (dz_vals * conv).astype(jnp.bfloat16)
    grad_conv = rounded(dz_vals * query_proj.astype(jnp.float32))
    grad_ext = jnp.concatenate([grad_conv, zero_rows], 0)

    def back_step(block_index, carry):
        grad_all, filt_acc = carry
        first_row = (block_index * TAPS).astype(jnp.int32)
        window = lax.dynamic_slice_in_dim(mixed_ext, first_row, 2 * TAPS, 0)
        grad_window = lax.dynamic_slice_in_dim(grad_ext, first_row, 2 * TAPS, 0)
        grad_rows = lax.dynamic_slice_in_dim(grad_conv, first_row, TAPS, 0)
        ids_rows = lax.dynamic_slice_in_dim(ids_pad, first_row + TAPS, TAPS, 0)
        ids_prev = lax.dynamic_slice_in_dim(ids_pad, first_row, 2 * TAPS, 0)
        ids_next = lax.dynamic_slice_in_dim(ids_pad, first_row + TAPS, 2 * TAPS, 0)
        same_prev = (ids_rows[:, None] == ids_prev[None, :]).astype(jnp.float32)
        same_next = (ids_rows[:, None] == ids_next[None, :]).astype(jnp.float32)
        block_grad = jnp.einsum("gtw,wgc->tgc", back_table * same_next[None],
                                grad_window.reshape(2 * TAPS, GROUPS, GROUP_CH), precision=highest)
        product = jnp.einsum("tgc,wgc->gtw", grad_rows.reshape(TAPS, GROUPS, GROUP_CH),
                             window.reshape(2 * TAPS, GROUPS, GROUP_CH), precision=highest)
        filt_acc = filt_acc + fold_lags(product * same_prev[None], TAPS)
        grad_all = lax.dynamic_update_slice_in_dim(grad_all, block_grad.reshape(TAPS, D), first_row, 0)
        return grad_all, filt_acc

    grad_mixed, filter_grad = lax.fori_loop(
        0, TOKENS // TAPS, back_step,
        (jnp.zeros((TOKENS, D), jnp.float32), jnp.zeros((GROUPS, TAPS), jnp.float32)))
    key_grad = (grad_mixed * value_f32).astype(jnp.bfloat16)
    value_grad = (grad_mixed * key_f32).astype(jnp.bfloat16)
    return query_grad, key_grad, value_grad, filter_grad
```

```python
import jax
import jax.numpy as jnp
from jax import lax
from jax.experimental import pallas as pl
from jax.experimental.pallas import tpu as pltpu
from jax.sharding import PartitionSpec as P

BF = jnp.bfloat16
F32 = jnp.float32


def from_behind(array, axis, by):
    length = lax.axis_size(axis)
    pairs = [(i, i + by) for i in range(length) if 0 <= i + by < length]
    return lax.ppermute(array, axis, pairs)


def circulant(row, taps):
    wide = jnp.broadcast_to(row, (taps, taps))
    return pltpu.roll(wide, 0, 1, stride=1, stride_axis=0)


def pick_groups(stacked, taps, chans):
    lanes = lax.broadcasted_iota(jnp.int32, (taps, stacked.shape[1]), 1) // chans
    total = stacked[:taps]
    for i in range(1, stacked.shape[0] // taps):
        total = jnp.where(lanes == i, stacked[i * taps : (i + 1) * taps], total)
    return total


def fill_tables(table_ref, filt_ref, mask_ref, groups, taps):
    for i in range(groups):
        ring = circulant(filt_ref[i : i + 1, :], taps).astype(BF)
        rows = slice(i * taps, (i + 1) * taps)
        table_ref[rows, :taps] = ring * mask_ref[:, :taps]
        table_ref[rows, taps:] = ring * mask_ref[:, taps:]


def forward_kernel(filt_ref, mask_ref, before_ref, mixed_ref, conv_ref, table_ref):
    taps, width = mixed_ref.shape
    groups = filt_ref.shape[0]
    fill_tables(table_ref, filt_ref, mask_ref, groups, taps)
    window = jnp.concatenate([before_ref[...], mixed_ref[...]], 0)
    out = jnp.dot(table_ref[...], window, preferred_element_type=F32)
    conv_ref[...] = pick_groups(out, taps, width // groups)


def backward_kernel(
    filt_ref, back_ref, mask_ref, flip_ref, before_ref, mixed_ref, grad_ref, after_ref, key_ref, value_ref,
    key_out, value_out, filt_out, table_ref, rows_ref,
):
    taps, width = mixed_ref.shape
    groups = filt_ref.shape[0]
    chans = width // groups
    fill_tables(table_ref, filt_ref, back_ref, groups, taps)
    grad = grad_ref[...]
    window = jnp.concatenate([grad, after_ref[...]], 0)
    out = jnp.dot(table_ref[...], window, preferred_element_type=F32)
    total = pick_groups(out, taps, chans)
    key_out[...] = (total * value_ref[...].astype(F32)).astype(BF)
    value_out[...] = (total * key_ref[...].astype(F32)).astype(BF)
    lanes = lax.broadcasted_iota(jnp.int32, (taps, width), 1) // chans
    upturned = jnp.dot(flip_ref[...], grad, preferred_element_type=F32)
    for i in range(groups):
        only = jnp.where(lanes == i, upturned, jnp.zeros_like(upturned))
        rows_ref[i * taps : (i + 1) * taps, :] = only.astype(BF)
    mixed_window = jnp.concatenate([before_ref[...], mixed_ref[...]], 0)
    product = lax.dot_general(
        rows_ref[...], mixed_window, (((1,), (1,)), ((), ())), preferred_element_type=F32
    )
    prev = mask_ref[:, :taps].astype(F32)
    own = mask_ref[:, taps:].astype(F32)
    sums = []
    for i in range(groups):
        block = product[i * taps : (i + 1) * taps]
        folded = block[:, :taps] * prev + block[:, taps:] * own
        turned = pltpu.roll(folded, 0, 1, stride=1, stride_axis=0)
        sums.append(jnp.sum(turned, axis=0, keepdims=True))
    filt_out[...] = jnp.concatenate(sums, 0)


def turn_lanes(array):
    return jnp.roll(jnp.flip(array, 1), 1, axis=1)


def forward_conv(filt_turned, mask, before, mixed, width=128):
    taps, total = mixed.shape
    groups = filt_turned.shape[0] * width // total
    block = pl.BlockSpec((taps, width), lambda i: (0, i))
    return pl.pallas_call(
        forward_kernel,
        grid=(total // width,),
        in_specs=[
            pl.BlockSpec((groups, taps), lambda i: (i, 0)),
            pl.BlockSpec((taps, 2 * taps), lambda i: (0, 0)),
            block,
            block,
        ],
        out_specs=block,
        out_shape=jax.ShapeDtypeStruct((taps, total), F32),
        scratch_shapes=[pltpu.VMEM((groups * taps, 2 * taps), BF)],
        cost_estimate=pl.CostEstimate(
            flops=total * taps * taps * 64, bytes_accessed=total * taps * 8, transcendentals=0
        ),
    )(filt_turned, mask, before, mixed)


def backward_conv(filt, back, mask, before, mixed, grad, after, key, value, width=128):
    taps, total = mixed.shape
    groups = filt.shape[0] * width // total
    block = pl.BlockSpec((taps, width), lambda i: (0, i))
    rows = pl.BlockSpec((groups, taps), lambda i: (i, 0))
    flat = pl.BlockSpec((taps, 2 * taps), lambda i: (0, 0))
    out = jax.ShapeDtypeStruct((taps, total), BF)
    return pl.pallas_call(
        backward_kernel,
        grid=(total // width,),
        in_specs=[rows, flat, flat, pl.BlockSpec((taps, taps), lambda i: (0, 0))] + [block] * 6,
        out_specs=[block, block, rows],
        out_shape=[out, out, jax.ShapeDtypeStruct(filt.shape, F32)],
        scratch_shapes=[
            pltpu.VMEM((groups * taps, 2 * taps), BF),
            pltpu.VMEM((groups * taps, width), BF),
        ],
        cost_estimate=pl.CostEstimate(
            flops=total * taps * taps * 128, bytes_accessed=total * taps * 16, transcendentals=0
        ),
    )(filt, back, mask[::-1], jnp.eye(taps, dtype=BF)[::-1], before, mixed, grad, after, key, value)


def link_masks(genome_ids, first_row, taps):
    pad_ids = jnp.full((taps,), -1, jnp.int32)
    ids_pad = jnp.concatenate([pad_ids, genome_ids, pad_ids])
    ids = lax.dynamic_slice_in_dim(ids_pad, first_row, 3 * taps)
    prev, own, after = ids[:taps], ids[taps : 2 * taps], ids[2 * taps :]
    r = lax.broadcasted_iota(jnp.int32, (taps, taps), 0)
    w = lax.broadcasted_iota(jnp.int32, (taps, taps), 1)
    same = own[:, None] == own[None, :]
    ahead = jnp.concatenate(
        [(own[:, None] == prev[None, :]) & (w > r), same & (w <= r)], 1
    )
    back = jnp.concatenate(
        [same & (w >= r), (own[:, None] == after[None, :]) & (w < r)], 1
    )
    return ahead.astype(BF), back.astype(BF)


def per_device(query_proj, key_proj, value_proj, genome_ids, filters, out_weight, out_grad):
    taps = filters.shape[1]
    row_count = query_proj.shape[0]
    ahead, back = link_masks(genome_ids, lax.axis_index("ctx") * row_count, taps)
    mixed = (key_proj.astype(F32) * value_proj.astype(F32)).astype(BF)
    before = from_behind(mixed, "ctx", 1)
    filt = filters.astype(BF).astype(F32)
    grad_full = lax.all_gather(out_grad, "tp", axis=1, tiled=True)
    columns = lax.all_to_all(grad_full, "ctx", split_axis=1, concat_axis=0, tiled=True)
    dz_vals = lax.psum_scatter(
        lax.dot_general(
            columns, out_weight, (((1,), (1,)), ((), ())), preferred_element_type=F32
        ).astype(BF),
        "ctx",
        scatter_dimension=0,
        tiled=True,
    ).astype(F32)
    conv = forward_conv(turn_lanes(filt), ahead, before, mixed)
    query_grad = (dz_vals * conv).astype(BF)
    grad_conv = (dz_vals * query_proj.astype(F32)).astype(BF)
    after = from_behind(grad_conv, "ctx", -1)
    key_grad, value_grad, turned = backward_conv(
        filt, back, ahead, before, mixed, grad_conv, after, key_proj, value_proj
    )
    filter_grad = jnp.flip(lax.psum(turned.astype(BF), "ctx").astype(F32), 1)
    return (query_grad, key_grad, value_grad, filter_grad)


def solution(mesh):
    rows = P(("group", "ctx"), "tp")
    in_specs = (rows, rows, rows, P("group"), P("tp", None), P("tp", "ctx"), rows)
    out_specs = (rows, rows, rows, P(("group", "tp"), None))
    return jax.shard_map(
        per_device, mesh=mesh, in_specs=in_specs, out_specs=out_specs, check_vma=False
    )
```

```python
import functools
import jax
import jax.numpy as jnp
from jax import lax
from jax.experimental import pallas as pl
from jax.experimental.pallas import tpu as pltpu
from jax.sharding import PartitionSpec as P

BF = jnp.bfloat16
F32 = jnp.float32


def circulant(row, taps):
    wide = jnp.broadcast_to(row, (taps, taps))
    return pltpu.roll(wide, 0, 1, stride=1, stride_axis=0)


def pick_groups(stacked, taps, chans):
    lanes = lax.broadcasted_iota(jnp.int32, (taps, stacked.shape[1]), 1) // chans
    total = stacked[:taps]
    for i in range(1, stacked.shape[0] // taps):
        total = jnp.where(lanes == i, stacked[i * taps : (i + 1) * taps], total)
    return total


def fill_tables(table_ref, filt_ref, mask_ref, groups, taps):
    for i in range(groups):
        ring = circulant(filt_ref[i : i + 1, :], taps).astype(BF)
        rows = slice(i * taps, (i + 1) * taps)
        table_ref[rows, :taps] = ring * mask_ref[:, :taps]
        table_ref[rows, taps:] = ring * mask_ref[:, taps:]


def link_masks(genome_ids, first_row, taps):
    pad_ids = jnp.full((taps,), -1, jnp.int32)
    ids_pad = jnp.concatenate([pad_ids, genome_ids, pad_ids])
    ids = lax.dynamic_slice_in_dim(ids_pad, first_row, 3 * taps)
    prev, own, after = ids[:taps], ids[taps : 2 * taps], ids[2 * taps :]
    r = lax.broadcasted_iota(jnp.int32, (taps, taps), 0)
    w = lax.broadcasted_iota(jnp.int32, (taps, taps), 1)
    same = own[:, None] == own[None, :]
    ahead = jnp.concatenate(
        [(own[:, None] == prev[None, :]) & (w > r), same & (w <= r)], 1
    )
    back = jnp.concatenate(
        [same & (w >= r), (own[:, None] == after[None, :]) & (w < r)], 1
    )
    return ahead.astype(BF), back.astype(BF)


STREAMS = 4
BLOCK = 128
MESH = pl.DeviceIdType.MESH


def turn_lanes(array):
    return jnp.roll(jnp.flip(array, 1), 1, axis=1)


def ring_to_ctx(place, n):
    late = place // (n // 2)
    return (1 - late) * (2 * place) + late * (2 * (n - 1 - place) + 1)


def ctx_to_ring(ctx, n):
    odd = ctx % 2
    return (1 - odd) * (ctx // 2) + odd * (n - 1 - ctx // 2)


def step_kernel(
    n, turned_ref, filt_ref, ahead_ref, back_ref, upside_ref, flip_ref,
    query_hbm, key_hbm, value_hbm, weight_hbm, grad_hbm,
    query_out, key_out, value_out, filt_out,
    query_ref, key_ref, value_ref, weight_ref, cols_ref, ring_ref, part_ref,
    window_ref, gwin_ref, conv_ref, table_ref, rows_ref, fpart_ref, fin_ref,
    local_sem, a2a_send, a2a_recv, pass_send, pass_recv, own_send,
    ring_send, ring_recv, mixed_sem, halo_send, halo_recv,
    fold_send, fold_recv, share_send, share_recv,
):
    taps, total = query_ref.shape
    width = weight_ref.shape[1]
    held = grad_hbm.shape[1] // width
    chunk = total // STREAMS
    blocks = total // BLOCK
    groups = filt_ref.shape[0] // blocks
    chans = BLOCK // groups
    me = lax.axis_index("ctx")
    core = lax.axis_index("tp")
    place = ctx_to_ring(me, n)
    half_rows = taps // 2
    mine = filt_ref.shape[0] // n

    def remote(src, dst, send, recv, ctx, tp):
        return pltpu.make_async_remote_copy(
            src_ref=src, dst_ref=dst, send_sem=send, recv_sem=recv,
            device_id={"ctx": ctx, "tp": tp}, device_id_type=MESH,
        )

    loads = [
        pltpu.make_async_copy(src, dst, local_sem.at[i])
        for i, (src, dst) in enumerate([
            (key_hbm, key_ref), (value_hbm, value_ref), (weight_hbm, weight_ref),
            (query_hbm, query_ref),
        ])
    ]
    for load in loads:
        load.start()

    barrier = pltpu.get_barrier_semaphore()
    for gap in range(n):
        for other in range(2):
            if gap or other:
                pl.semaphore_signal(
                    barrier, inc=1,
                    device_id={"ctx": (me + gap) % n, "tp": (core + other) % 2},
                    device_id_type=MESH,
                )
    pl.semaphore_wait(barrier, 2 * n - 1)

    def at_gap(gap):
        return ring_to_ctx((place + gap + n) % n, n)

    def columns_of(ctx):
        return pl.ds(pl.multiple_of((ctx % held) * width, width), width)

    def send_block(gap, half):
        ctx = at_gap(gap)
        rows = pl.ds(half * half_rows, half_rows)
        return ctx, remote(
            grad_hbm.at[rows, columns_of(ctx)], cols_ref.at[me, rows, :],
            a2a_send.at[gap % n, half], a2a_recv.at[me], ctx, half,
        )

    gaps = []
    for d in range(1, n // 2 + 1):
        gaps += [d, -d] if d < n // 2 else [d]

    def each_send(act):
        for gap in gaps:
            @pl.when(at_gap(gap) // held == core)
            def _(gap=gap):
                for half in range(2):
                    act(send_block(gap, half)[1])

    own_local = pltpu.make_async_copy(
        grad_hbm.at[:, columns_of(me)], cols_ref.at[me], local_sem.at[4]
    )
    own_remote = remote(
        grad_hbm.at[:, columns_of(me)], cols_ref.at[me],
        own_send, pass_recv.at[me], me, 1 - core,
    )
    each_send(lambda copy: copy.start())

    @pl.when(me // held == core)
    def _():
        own_local.start()
        own_remote.start()

    loads[0].wait()
    loads[1].wait()
    window_ref[taps:, :] = (
        key_ref[...].astype(F32) * value_ref[...].astype(F32)
    ).astype(BF)
    mixed_copy = remote(
        window_ref.at[pl.ds(taps, taps), :], window_ref.at[pl.ds(0, taps), :],
        mixed_sem.at[0], mixed_sem.at[1], (me + 1) % n, core,
    )

    @pl.when(me < n - 1)
    def _():
        mixed_copy.start()

    @pl.when(me == 0)
    def _():
        window_ref[:taps, :] = jnp.zeros((taps, total), BF)

    def passing(ctx, half):
        rows = pl.ds(pl.multiple_of(half * half_rows, half_rows), half_rows)
        spot = cols_ref.at[ctx, rows, :]
        return remote(spot, spot, pass_send.at[ctx], pass_recv.at[ctx], me, 1 - core)

    def arrived(ctx):
        rows = pl.ds(pl.multiple_of(core * half_rows, half_rows), half_rows)
        spot = cols_ref.at[ctx, rows, :]
        remote(spot, spot, pass_send.at[ctx], a2a_recv.at[ctx], me, 1 - core).wait_recv()

    def pass_on(d):
        def one(gap):
            ctx = at_gap(gap)
            arrived(ctx)
            passing(ctx, core).start()

        one(-1 - d)

        @pl.when(d < n // 2 - 1)
        def _():
            one(1 + d)

    def passed(d):
        passing(at_gap(-1 - d), 1 - core).wait_recv()

        @pl.when(d < n // 2 - 1)
        def _():
            passing(at_gap(1 + d), 1 - core).wait_recv()

    def block_lanes(i):
        return pl.ds(pl.multiple_of(i * BLOCK, BLOCK), BLOCK)

    def block_groups(i):
        return pl.ds(pl.multiple_of(i * groups, groups), groups)

    def conv_block(i):
        fill_tables(table_ref, turned_ref[block_groups(i), :], ahead_ref, groups, taps)
        out = jnp.dot(
            table_ref[...], window_ref[:, block_lanes(i)], preferred_element_type=F32
        )
        conv_ref[:, block_lanes(i)] = pick_groups(out, taps, chans)

    def ring_copy(k, step):
        gap = 1 if k % 2 == 0 else -1
        return remote(
            ring_ref.at[k, step], ring_ref.at[k, step + 1],
            ring_send.at[k, step], ring_recv.at[k, step + 1], at_gap(gap), core,
        )

    def ring_arrival(k, step):
        gap = 1 if k % 2 == 0 else -1
        return remote(
            ring_ref.at[k, step], ring_ref.at[k, step],
            ring_send.at[k, step], ring_recv.at[k, step], at_gap(gap), core,
        )

    def multiply(k, step):
        gap = -1 - step if k % 2 == 0 else 1 + step
        rows = cols_ref[ring_to_ctx((place + gap + 2 * n) % n, n)]
        part_ref[...] = lax.dot_general(
            rows, weight_ref[pl.ds(k * chunk, chunk), :], (((1,), (1,)), ((), ())),
            preferred_element_type=F32,
        ).astype(BF)

    pass_on(0)
    loads[2].wait()
    slots = (n - 2) * STREAMS

    def ring_step(step, carry):
        @pl.when(step < n // 2)
        def _():
            passed(step)

        @pl.when((step == 1) & (me > 0))
        def _():
            mixed_copy.wait_recv()

        for k in range(STREAMS):
            multiply(k, step)

            @pl.when(step == 0)
            def _(k=k):
                ring_ref[k, step] = part_ref[...]

            @pl.when(step > 0)
            def _(k=k):
                ring_arrival(k, step).wait_recv()
                ring_ref[k, step] = (
                    ring_ref[k, step].astype(F32) + part_ref[...].astype(F32)
                ).astype(BF)

            ring_copy(k, step).start()

            @pl.when(step > 0)
            def _(k=k):
                slot = (step - 1) * STREAMS + k
                lax.fori_loop(
                    slot * blocks // slots, (slot + 1) * blocks // slots,
                    lambda i, c: (conv_block(i), c)[1], 0,
                )

        @pl.when(step + 1 < n // 2)
        def _():
            pass_on(step + 1)

        return carry

    lax.fori_loop(0, n - 1, ring_step, 0)

    @pl.when(me // held == core)
    def _():
        own_local.wait()
        own_remote.wait_send()

    @pl.when(me // held != core)
    def _():
        own_remote.wait_recv()

    loads[3].wait()

    @pl.when(me == n - 1)
    def _():
        gwin_ref[taps:, :] = jnp.zeros((taps, total), BF)

    def halo_copy(k):
        cols = pl.ds(k * chunk, chunk)
        return remote(
            gwin_ref.at[pl.ds(0, taps), cols], gwin_ref.at[pl.ds(taps, taps), cols],
            halo_send.at[k], halo_recv.at[k], (me + n - 1) % n, core,
        )

    for k in range(STREAMS):
        cols = pl.ds(k * chunk, chunk)
        multiply(k, n - 1)
        ring_arrival(k, n - 1).wait_recv()
        dz = ring_ref[k, n - 1].astype(F32) + part_ref[...].astype(F32)
        dz = dz.astype(BF).astype(F32)
        gwin_ref[:taps, cols] = (dz * query_ref[:, cols].astype(F32)).astype(BF)

        @pl.when(me > 0)
        def _(k=k):
            halo_copy(k).start()

        query_out[:, cols] = (dz * conv_ref[:, cols]).astype(BF)

    prev = upside_ref[:, :taps].astype(F32)
    own = upside_ref[:, taps:].astype(F32)
    lanes = lax.broadcasted_iota(jnp.int32, (taps, BLOCK), 1) // chans

    def filter_block(i, carry):
        upturned = jnp.dot(
            flip_ref[...], gwin_ref[:taps, block_lanes(i)], preferred_element_type=F32
        )
        for g in range(groups):
            only = jnp.where(lanes == g, upturned, jnp.zeros_like(upturned))
            rows_ref[g * taps : (g + 1) * taps, :] = only.astype(BF)
        product = lax.dot_general(
            rows_ref[...], window_ref[:, block_lanes(i)], (((1,), (1,)), ((), ())),
            preferred_element_type=F32,
        )
        sums = []
        for g in range(groups):
            block = product[g * taps : (g + 1) * taps]
            folded = block[:, :taps] * prev + block[:, taps:] * own
            moved = pltpu.roll(folded, 0, 1, stride=1, stride_axis=0)
            sums.append(jnp.sum(moved, axis=0, keepdims=True))
        fpart_ref[block_groups(i), :] = jnp.concatenate(sums, 0)
        return carry

    lax.fori_loop(0, blocks, filter_block, 0)

    def slice_of(ctx):
        return pl.ds(pl.multiple_of(ctx * mine, mine), mine)

    def fold_copy(gap):
        ctx = (me + gap) % n
        return remote(
            fpart_ref.at[slice_of(ctx), :], fin_ref.at[gap],
            fold_send.at[gap], fold_recv.at[gap], ctx, core,
        )

    def share_copy(gap):
        return remote(
            filt_out.at[slice_of(me), :], filt_out.at[slice_of(me), :],
            share_send.at[gap], share_recv.at[gap], (me + gap) % n, core,
        )

    for gap in range(1, n):
        fold_copy(gap).start()

    def backward_block(i, carry):
        fill_tables(table_ref, filt_ref[block_groups(i), :], back_ref, groups, taps)
        out = jnp.dot(
            table_ref[...], gwin_ref[:, block_lanes(i)], preferred_element_type=F32
        )
        grad = pick_groups(out, taps, chans)
        cols = block_lanes(i)
        key_out[:, cols] = (grad * value_ref[:, cols].astype(F32)).astype(BF)
        value_out[:, cols] = (grad * key_ref[:, cols].astype(F32)).astype(BF)
        return carry

    for k in range(STREAMS):
        @pl.when(me < n - 1)
        def _(k=k):
            halo_copy(k).wait_recv()

        lax.fori_loop(k * blocks // STREAMS, (k + 1) * blocks // STREAMS, backward_block, 0)
        if k == STREAMS - 2:
            summed = fpart_ref[slice_of(me), :]
            for gap in range(1, n):
                fold_copy(gap).wait_recv()
                summed = summed + fin_ref[gap]
            filt_out[slice_of(me), :] = summed
            for gap in range(1, n):
                share_copy(gap).start()

    for gap in range(1, n):
        sender = (me + n - gap) % n
        remote(
            filt_out.at[slice_of(sender), :], filt_out.at[slice_of(sender), :],
            share_send.at[gap], share_recv.at[gap], sender, core,
        ).wait_recv()

    each_send(lambda copy: copy.wait_send())
    for gap in gaps:
        passing(at_gap(gap), core).wait_send()

    @pl.when(me < n - 1)
    def _():
        mixed_copy.wait_send()

    for k in range(STREAMS):
        for step in range(n - 1):
            ring_copy(k, step).wait_send()

        @pl.when(me > 0)
        def _(k=k):
            halo_copy(k).wait_send()

    for gap in range(1, n):
        fold_copy(gap).wait_send()
        share_copy(gap).wait_send()


def per_device(query_proj, key_proj, value_proj, genome_ids, filters, out_weight, out_grad):
    taps = filters.shape[1]
    n = lax.axis_size("ctx")
    row_count, total = query_proj.shape
    width = out_weight.shape[1]
    groups = filters.shape[0] * BLOCK // total
    ahead, back = link_masks(genome_ids, lax.axis_index("ctx") * row_count, taps)
    filt = filters.astype(BF).astype(F32)
    out = jax.ShapeDtypeStruct((row_count, total), BF)
    vmem = pl.BlockSpec(memory_space=pltpu.VMEM)
    anywhere = pl.BlockSpec(memory_space=pl.ANY)
    dma = pltpu.SemaphoreType.DMA
    query_grad, key_grad, value_grad, filter_grad = pl.pallas_call(
        functools.partial(step_kernel, n),
        in_specs=[vmem] * 6 + [anywhere] * 5,
        out_specs=[vmem] * 4,
        out_shape=[out, out, out, jax.ShapeDtypeStruct(filt.shape, F32)],
        scratch_shapes=[
            pltpu.VMEM((row_count, total), BF),
            pltpu.VMEM((row_count, total), BF),
            pltpu.VMEM((row_count, total), BF),
            pltpu.VMEM(out_weight.shape, BF),
            pltpu.VMEM((n, row_count, width), BF),
            pltpu.VMEM((STREAMS, n, row_count, total // STREAMS), BF),
            pltpu.VMEM((row_count, total // STREAMS), BF),
            pltpu.VMEM((2 * taps, total), BF),
            pltpu.VMEM((2 * taps, total), BF),
            pltpu.VMEM((row_count, total), F32),
            pltpu.VMEM((groups * taps, 2 * taps), BF),
            pltpu.VMEM((groups * taps, BLOCK), BF),
            pltpu.VMEM(filt.shape, F32),
            pltpu.VMEM((n, filt.shape[0] // n, taps), F32),
            dma((5,)), dma((n, 2)), dma((n,)), dma((n,)), dma((n,)), dma,
            dma((STREAMS, n)), dma((STREAMS, n)), dma((2,)), dma((STREAMS,)), dma((STREAMS,)),
            dma((n,)), dma((n,)), dma((n,)), dma((n,)),
        ],
        compiler_params=pltpu.CompilerParams(
            collective_id=0, has_side_effects=True, vmem_limit_bytes=56 * 1024 * 1024
        ),
    )(
        turn_lanes(filt), filt, ahead, back, ahead[::-1], jnp.eye(taps, dtype=BF)[::-1],
        query_proj, key_proj, value_proj, out_weight, out_grad,
    )
    return (query_grad, key_grad, value_grad, jnp.flip(filter_grad, 1))


def solution(mesh):
    rows = P(("group", "ctx"), "tp")
    in_specs = (rows, rows, rows, P("group"), P("tp", None), P("tp", "ctx"), rows)
    out_specs = (rows, rows, rows, P(("group", "tp"), None))
    return jax.shard_map(
        per_device, mesh=mesh, in_specs=in_specs, out_specs=out_specs, check_vma=False
    )
```

```python
import functools
import jax
import jax.numpy as jnp
from jax import lax
from jax.experimental import pallas as pl
from jax.experimental.pallas import tpu as pltpu
from jax.sharding import PartitionSpec as P

BF = jnp.bfloat16
F32 = jnp.float32


def circulant(row, taps):
    wide = jnp.broadcast_to(row, (taps, taps))
    return pltpu.roll(wide, 0, 1, stride=1, stride_axis=0)


def pick_groups(stacked, taps, chans):
    lanes = lax.broadcasted_iota(jnp.int32, (taps, stacked.shape[1]), 1) // chans
    total = stacked[:taps]
    for i in range(1, stacked.shape[0] // taps):
        total = jnp.where(lanes == i, stacked[i * taps : (i + 1) * taps], total)
    return total


def fill_tables(table_ref, filt_ref, mask_ref, groups, taps):
    for i in range(groups):
        ring = circulant(filt_ref[i : i + 1, :], taps).astype(BF)
        rows = slice(i * taps, (i + 1) * taps)
        table_ref[rows, :taps] = ring * mask_ref[:, :taps]
        table_ref[rows, taps:] = ring * mask_ref[:, taps:]


def link_masks(genome_ids, first_row, taps):
    pad_ids = jnp.full((taps,), -1, jnp.int32)
    ids_pad = jnp.concatenate([pad_ids, genome_ids, pad_ids])
    ids = lax.dynamic_slice_in_dim(ids_pad, first_row, 3 * taps)
    prev, own, after = ids[:taps], ids[taps : 2 * taps], ids[2 * taps :]
    r = lax.broadcasted_iota(jnp.int32, (taps, taps), 0)
    w = lax.broadcasted_iota(jnp.int32, (taps, taps), 1)
    same = own[:, None] == own[None, :]
    ahead = jnp.concatenate(
        [(own[:, None] == prev[None, :]) & (w > r), same & (w <= r)], 1
    )
    back = jnp.concatenate(
        [same & (w >= r), (own[:, None] == after[None, :]) & (w < r)], 1
    )
    return ahead.astype(BF), back.astype(BF)


STREAMS = 4
BLOCK = 128
MESH = pl.DeviceIdType.MESH


def turn_lanes(array):
    return jnp.roll(jnp.flip(array, 1), 1, axis=1)


def ring_to_ctx(place, n):
    late = place // (n // 2)
    return (1 - late) * (2 * place) + late * (2 * (n - 1 - place) + 1)


def ctx_to_ring(ctx, n):
    odd = ctx % 2
    return (1 - odd) * (ctx // 2) + odd * (n - 1 - ctx // 2)


def step_kernel(
    n, turned_ref, filt_ref, ahead_ref, back_ref,
    query_hbm, key_hbm, value_hbm, weight_hbm, grad_hbm,
    query_out, key_out, value_out, filt_out,
    query_ref, key_ref, value_ref, weight_ref, cols_ref, ring_ref, part_ref,
    window_ref, gwin_ref, conv_ref, table_ref, tables_ref, rows_ref, fpart_ref, fin_ref,
    local_sem, a2a_send, a2a_recv, pass_send, pass_recv, own_send,
    ring_send, ring_recv, mixed_sem, halo_send, halo_recv,
    fold_send, fold_recv, share_send, share_recv,
):
    taps, total = query_ref.shape
    width = weight_ref.shape[1]
    held = grad_hbm.shape[1] // width
    chunk = total // STREAMS
    blocks = total // BLOCK
    groups = filt_ref.shape[0] // blocks
    chans = BLOCK // groups
    me = lax.axis_index("ctx")
    core = lax.axis_index("tp")
    place = ctx_to_ring(me, n)
    half_rows = taps // 2
    mine = filt_ref.shape[0] // n

    def remote(src, dst, send, recv, ctx, tp):
        return pltpu.make_async_remote_copy(
            src_ref=src, dst_ref=dst, send_sem=send, recv_sem=recv,
            device_id={"ctx": ctx, "tp": tp}, device_id_type=MESH,
        )

    loads = [
        pltpu.make_async_copy(src, dst, local_sem.at[i])
        for i, (src, dst) in enumerate([
            (key_hbm, key_ref), (value_hbm, value_ref), (weight_hbm, weight_ref),
            (query_hbm, query_ref),
        ])
    ]
    for load in loads:
        load.start()

    barrier = pltpu.get_barrier_semaphore()
    for gap in range(n):
        for other in range(2):
            if gap or other:
                pl.semaphore_signal(
                    barrier, inc=1,
                    device_id={"ctx": (me + gap) % n, "tp": (core + other) % 2},
                    device_id_type=MESH,
                )
    pl.semaphore_wait(barrier, 2 * n - 1)

    def at_gap(gap):
        return ring_to_ctx((place + gap + n) % n, n)

    def columns_of(ctx):
        return pl.ds(pl.multiple_of((ctx % held) * width, width), width)

    def send_block(gap, half):
        ctx = at_gap(gap)
        rows = pl.ds(half * half_rows, half_rows)
        return ctx, remote(
            grad_hbm.at[rows, columns_of(ctx)], cols_ref.at[me, rows, :],
            a2a_send.at[gap % n, half], a2a_recv.at[me], ctx, half,
        )

    gaps = []
    for d in range(1, n // 2 + 1):
        gaps += [d, -d] if d < n // 2 else [d]

    def each_send(act):
        for gap in gaps:
            @pl.when(at_gap(gap) // held == core)
            def _(gap=gap):
                for half in range(2):
                    act(send_block(gap, half)[1])

    own_local = pltpu.make_async_copy(
        grad_hbm.at[:, columns_of(me)], cols_ref.at[me], local_sem.at[4]
    )
    own_remote = remote(
        grad_hbm.at[:, columns_of(me)], cols_ref.at[me],
        own_send, pass_recv.at[me], me, 1 - core,
    )
    each_send(lambda copy: copy.start())

    @pl.when(me // held == core)
    def _():
        own_local.start()
        own_remote.start()

    loads[0].wait()
    loads[1].wait()
    window_ref[taps:, :] = (
        key_ref[...].astype(F32) * value_ref[...].astype(F32)
    ).astype(BF)
    mixed_copy = remote(
        window_ref.at[pl.ds(taps, taps), :], window_ref.at[pl.ds(0, taps), :],
        mixed_sem.at[0], mixed_sem.at[1], (me + 1) % n, core,
    )

    @pl.when(me < n - 1)
    def _():
        mixed_copy.start()

    @pl.when(me == 0)
    def _():
        window_ref[:taps, :] = jnp.zeros((taps, total), BF)

    def passing(ctx, half):
        rows = pl.ds(pl.multiple_of(half * half_rows, half_rows), half_rows)
        spot = cols_ref.at[ctx, rows, :]
        return remote(spot, spot, pass_send.at[ctx], pass_recv.at[ctx], me, 1 - core)

    def arrived(ctx):
        rows = pl.ds(pl.multiple_of(core * half_rows, half_rows), half_rows)
        spot = cols_ref.at[ctx, rows, :]
        remote(spot, spot, pass_send.at[ctx], a2a_recv.at[ctx], me, 1 - core).wait_recv()

    def pass_on(d):
        def one(gap):
            ctx = at_gap(gap)
            arrived(ctx)
            passing(ctx, core).start()

        one(-1 - d)

        @pl.when(d < n // 2 - 1)
        def _():
            one(1 + d)

    def passed(d):
        passing(at_gap(-1 - d), 1 - core).wait_recv()

        @pl.when(d < n // 2 - 1)
        def _():
            passing(at_gap(1 + d), 1 - core).wait_recv()

    def block_lanes(i):
        return pl.ds(pl.multiple_of(i * BLOCK, BLOCK), BLOCK)

    def block_groups(i):
        return pl.ds(pl.multiple_of(i * groups, groups), groups)

    def conv_block(i):
        fill_tables(table_ref, turned_ref[block_groups(i), :], ahead_ref, groups, taps)
        out = jnp.dot(
            table_ref[...], window_ref[:, block_lanes(i)], preferred_element_type=F32
        )
        conv_ref[:, block_lanes(i)] = pick_groups(out, taps, chans)

    def back_table(i):
        fill_tables(
            tables_ref.at[i], filt_ref[block_groups(i), :], back_ref, groups, taps
        )

    def ring_copy(k, step):
        gap = 1 if k % 2 == 0 else -1
        return remote(
            ring_ref.at[k, step], ring_ref.at[k, step + 1],
            ring_send.at[k, step], ring_recv.at[k, step + 1], at_gap(gap), core,
        )

    def ring_arrival(k, step):
        gap = 1 if k % 2 == 0 else -1
        return remote(
            ring_ref.at[k, step], ring_ref.at[k, step],
            ring_send.at[k, step], ring_recv.at[k, step], at_gap(gap), core,
        )

    def multiply(k, step):
        gap = -1 - step if k % 2 == 0 else 1 + step
        rows = cols_ref[ring_to_ctx((place + gap + 2 * n) % n, n)]
        part_ref[...] = lax.dot_general(
            rows, weight_ref[pl.ds(k * chunk, chunk), :], (((1,), (1,)), ((), ())),
            preferred_element_type=F32,
        ).astype(BF)

    pass_on(0)
    loads[2].wait()
    slots = (n - 2) * STREAMS
    turns = (n - 1) * STREAMS

    def ring_step(step, carry):
        @pl.when(step < n // 2)
        def _():
            passed(step)

        @pl.when((step == 1) & (me > 0))
        def _():
            mixed_copy.wait_recv()

        for k in range(STREAMS):
            multiply(k, step)

            @pl.when(step == 0)
            def _(k=k):
                ring_ref[k, step] = part_ref[...]

            @pl.when(step > 0)
            def _(k=k):
                ring_arrival(k, step).wait_recv()
                ring_ref[k, step] = (
                    ring_ref[k, step].astype(F32) + part_ref[...].astype(F32)
                ).astype(BF)

            ring_copy(k, step).start()
            turn = step * STREAMS + k
            lax.fori_loop(
                turn * blocks // turns, (turn + 1) * blocks // turns,
                lambda i, c: (back_table(i), c)[1], 0,
            )

            @pl.when(step > 0)
            def _(k=k):
                slot = (step - 1) * STREAMS + k
                lax.fori_loop(
                    slot * blocks // slots, (slot + 1) * blocks // slots,
                    lambda i, c: (conv_block(i), c)[1], 0,
                )

        @pl.when(step + 1 < n // 2)
        def _():
            pass_on(step + 1)

        return carry

    lax.fori_loop(0, n - 1, ring_step, 0)

    @pl.when(me // held == core)
    def _():
        own_local.wait()
        own_remote.wait_send()

    @pl.when(me // held != core)
    def _():
        own_remote.wait_recv()

    loads[3].wait()

    @pl.when(me == n - 1)
    def _():
        gwin_ref[taps:, :] = jnp.zeros((taps, total), BF)

    def halo_copy(k):
        cols = pl.ds(k * chunk, chunk)
        return remote(
            gwin_ref.at[pl.ds(0, taps), cols], gwin_ref.at[pl.ds(taps, taps), cols],
            halo_send.at[k], halo_recv.at[k], (me + n - 1) % n, core,
        )

    for k in range(STREAMS):
        cols = pl.ds(k * chunk, chunk)
        multiply(k, n - 1)
        ring_arrival(k, n - 1).wait_recv()
        dz = ring_ref[k, n - 1].astype(F32) + part_ref[...].astype(F32)
        dz = dz.astype(BF).astype(F32)
        gwin_ref[:taps, cols] = (dz * query_ref[:, cols].astype(F32)).astype(BF)

        @pl.when(me > 0)
        def _(k=k):
            halo_copy(k).start()

        query_out[:, cols] = (dz * conv_ref[:, cols]).astype(BF)

    down = lax.broadcasted_iota(jnp.int32, (taps, taps), 0)
    across = lax.broadcasted_iota(jnp.int32, (taps, taps), 1)
    flip = jnp.where(down + across == taps - 1, 1.0, 0.0).astype(BF)
    upside = jnp.dot(flip, ahead_ref[...], preferred_element_type=F32)
    prev = upside[:, :taps]
    own = upside[:, taps:]
    lanes = lax.broadcasted_iota(jnp.int32, (taps, BLOCK), 1) // chans

    def filter_block(i, carry):
        upturned = jnp.dot(
            flip, gwin_ref[:taps, block_lanes(i)], preferred_element_type=F32
        )
        for g in range(groups):
            only = jnp.where(lanes == g, upturned, jnp.zeros_like(upturned))
            rows_ref[g * taps : (g + 1) * taps, :] = only.astype(BF)
        product = lax.dot_general(
            rows_ref[...], window_ref[:, block_lanes(i)], (((1,), (1,)), ((), ())),
            preferred_element_type=F32,
        )
        sums = []
        for g in range(groups):
            block = product[g * taps : (g + 1) * taps]
            folded = block[:, :taps] * prev + block[:, taps:] * own
            moved = pltpu.roll(folded, 0, 1, stride=1, stride_axis=0)
            sums.append(jnp.sum(moved, axis=0, keepdims=True))
        fpart_ref[block_groups(i), :] = jnp.concatenate(sums, 0)
        return carry

    lax.fori_loop(0, blocks, filter_block, 0)

    def slice_of(ctx):
        return pl.ds(pl.multiple_of(ctx * mine, mine), mine)

    def fold_copy(gap):
        ctx = (me + gap) % n
        return remote(
            fpart_ref.at[slice_of(ctx), :], fin_ref.at[gap],
            fold_send.at[gap], fold_recv.at[gap], ctx, core,
        )

    def share_copy(gap):
        return remote(
            filt_out.at[slice_of(me), :], filt_out.at[slice_of(me), :],
            share_send.at[gap], share_recv.at[gap], (me + gap) % n, core,
        )

    for gap in range(1, n):
        fold_copy(gap).start()

    def backward_block(i, carry):
        out = jnp.dot(
            tables_ref[i], gwin_ref[:, block_lanes(i)], preferred_element_type=F32
        )
        grad = pick_groups(out, taps, chans)
        cols = block_lanes(i)
        key_out[:, cols] = (grad * value_ref[:, cols].astype(F32)).astype(BF)
        value_out[:, cols] = (grad * key_ref[:, cols].astype(F32)).astype(BF)
        return carry

    for k in range(STREAMS):
        @pl.when(me < n - 1)
        def _(k=k):
            halo_copy(k).wait_recv()

        lax.fori_loop(k * blocks // STREAMS, (k + 1) * blocks // STREAMS, backward_block, 0)
        if k == STREAMS - 2:
            summed = fpart_ref[slice_of(me), :]
            for gap in range(1, n):
                fold_copy(gap).wait_recv()
                summed = summed + fin_ref[gap]
            filt_out[slice_of(me), :] = summed
            for gap in range(1, n):
                share_copy(gap).start()

    for gap in range(1, n):
        sender = (me + n - gap) % n
        remote(
            filt_out.at[slice_of(sender), :], filt_out.at[slice_of(sender), :],
            share_send.at[gap], share_recv.at[gap], sender, core,
        ).wait_recv()

    each_send(lambda copy: copy.wait_send())
    for gap in gaps:
        passing(at_gap(gap), core).wait_send()

    @pl.when(me < n - 1)
    def _():
        mixed_copy.wait_send()

    for k in range(STREAMS):
        for step in range(n - 1):
            ring_copy(k, step).wait_send()

        @pl.when(me > 0)
        def _(k=k):
            halo_copy(k).wait_send()

    for gap in range(1, n):
        fold_copy(gap).wait_send()
        share_copy(gap).wait_send()


def per_device(query_proj, key_proj, value_proj, genome_ids, filters, out_weight, out_grad):
    taps = filters.shape[1]
    n = lax.axis_size("ctx")
    row_count, total = query_proj.shape
    width = out_weight.shape[1]
    groups = filters.shape[0] * BLOCK // total
    ahead, back = link_masks(genome_ids, lax.axis_index("ctx") * row_count, taps)
    filt = filters.astype(BF).astype(F32)
    out = jax.ShapeDtypeStruct((row_count, total), BF)
    vmem = pl.BlockSpec(memory_space=pltpu.VMEM)
    anywhere = pl.BlockSpec(memory_space=pl.ANY)
    dma = pltpu.SemaphoreType.DMA
    query_grad, key_grad, value_grad, filter_grad = pl.pallas_call(
        functools.partial(step_kernel, n),
        in_specs=[vmem] * 4 + [anywhere] * 5,
        out_specs=[vmem] * 4,
        out_shape=[out, out, out, jax.ShapeDtypeStruct(filt.shape, F32)],
        scratch_shapes=[
            pltpu.VMEM((row_count, total), BF),
            pltpu.VMEM((row_count, total), BF),
            pltpu.VMEM((row_count, total), BF),
            pltpu.VMEM(out_weight.shape, BF),
            pltpu.VMEM((n, row_count, width), BF),
            pltpu.VMEM((STREAMS, n, row_count, total // STREAMS), BF),
            pltpu.VMEM((row_count, total // STREAMS), BF),
            pltpu.VMEM((2 * taps, total), BF),
            pltpu.VMEM((2 * taps, total), BF),
            pltpu.VMEM((row_count, total), F32),
            pltpu.VMEM((groups * taps, 2 * taps), BF),
            pltpu.VMEM((total // BLOCK, groups * taps, 2 * taps), BF),
            pltpu.VMEM((groups * taps, BLOCK), BF),
            pltpu.VMEM(filt.shape, F32),
            pltpu.VMEM((n, filt.shape[0] // n, taps), F32),
            dma((5,)), dma((n, 2)), dma((n,)), dma((n,)), dma((n,)), dma,
            dma((STREAMS, n)), dma((STREAMS, n)), dma((2,)), dma((STREAMS,)), dma((STREAMS,)),
            dma((n,)), dma((n,)), dma((n,)), dma((n,)),
        ],
        compiler_params=pltpu.CompilerParams(
            collective_id=0, has_side_effects=True, vmem_limit_bytes=60 * 1024 * 1024
        ),
    )(
        turn_lanes(filt), filt, ahead, back,
        query_proj, key_proj, value_proj, out_weight, out_grad,
    )
    return (query_grad, key_grad, value_grad, jnp.flip(filter_grad, 1))


def solution(mesh):
    rows = P(("group", "ctx"), "tp")
    in_specs = (rows, rows, rows, P("group"), P("tp", None), P("tp", "ctx"), rows)
    out_specs = (rows, rows, rows, P(("group", "tp"), None))
    return jax.shard_map(
        per_device, mesh=mesh, in_specs=in_specs, out_specs=out_specs, check_vma=False
    )
```
